32 devices in a mesh: leaf: 8 (over z, y), rep: 4 (over x, core).
Axes of the slice: x: 2, y: 2, z: 4, core: 2. Of those that a mesh axis runs over, the one named last changes fastest.
Arguments:
- coords: float32 [8, 8192], P(None, 'leaf'), may hold values from -8 to 8
- skeleton: float32 [8, 1024], P(None, 'leaf'), may hold values from -8 to 8
- transfer: bfloat16 [16, 64, 64], P('leaf'), may hold values from -0.75 to 0.75
- coupling: bfloat16 [256, 256], replicated, may hold values from -3 to 3, as said below
- parent: int32 [16], P('leaf'), may hold values from 0 to 3, never falling along the last dimension, each value on 1 to 6 neighbouring positions
- near_mask: int32 [16, 5], P('leaf'), may hold values from 0 to 1, as said below
- noise: float32 [8192], P('leaf'), may hold values from 0.5 to 2
- rhs: float32 [64, 8192], P('rep', 'leaf'), may hold values from -5 to 5
Outputs:
- solution: float32 [64, 8192], P('rep', 'leaf')
- residual: float32 [64, 8192], P('rep', 'leaf')
The draws below stay inside these ranges and needn't reach their ends.
Inputs may be any that keep to these rules, and one draw needn't show every extreme that they name: `coupling`: symmetric positive semidefinite. `parent`: never falling along the leaves. Slot 2 is 1; near_mask[l, 2 + o] = near_mask[l + o, 2 - o]; slots pointing before the first or after the last leaf are 0.
All inputs are finite; a program needn't handle non-finite values.
Results may differ from the reference program's by a relative error of at most 0.0003.
Values sent between devices are 32-bit elements; how exact they have to be, the bound alone decides.
A program may use at most 64 MiB of HBM per device.

```python
import math
import jax
import jax.numpy as jnp
import numpy as np
from jax import lax

LEAF = 512
DIM = 8
RANK = 64
NRHS = 64
ITERS = 2
LEAF_DEV = 2
REACH = 2
LEAVES = 16
POINTS = 8192
LEVEL2 = 4
CHILD_MOST = 6


def leaf_centers(key):
    slopes = jax.random.uniform(jax.random.fold_in(key, 11), (DIM, 1), minval=0.1, maxval=0.25)
    phases = jax.random.uniform(jax.random.fold_in(key, 12), (DIM, 1), minval=-3.1, maxval=3.1)
    positions = jnp.arange(LEAVES, dtype=jnp.float32)[None, :]
    return 5.0 * jnp.sin(slopes * positions + phases)


def point_cloud(key):
    centers = leaf_centers(key)
    spread = jnp.clip(jax.random.normal(jax.random.fold_in(key, 13), (DIM, LEAVES, LEAF)), -3.0, 3.0)
    return (centers[:, :, None] + spread).reshape(DIM, LEAVES * LEAF)


def draw_coords(key, part):
    return point_cloud(key)


def draw_skeleton(key, part):
    centers = leaf_centers(key)
    spread = 0.8 * jnp.clip(jax.random.normal(jax.random.fold_in(key, 21), (DIM, LEAVES, RANK)), -3.0, 3.0)
    return (centers[:, :, None] + spread).reshape(DIM, LEAVES * RANK)


def draw_coupling(key, part):
    extent = LEVEL2 * RANK
    noise_part = jnp.clip(jax.random.normal(jax.random.fold_in(key, 31), (extent, extent)), -4.0, 4.0)
    factor = jnp.eye(extent, dtype=jnp.float32) + noise_part / jnp.sqrt(jnp.float32(extent))
    product = jnp.dot(factor, factor.T, precision=lax.Precision.HIGHEST)
    product = 0.5 * (product + product.T) / jnp.sqrt(jnp.float32(LEAVES // LEVEL2))
    return product.astype(jnp.bfloat16)


def draw_near_mask(key, part):
    crowded = jax.random.randint(jax.random.fold_in(key, 41), (LEAVES // LEAF_DEV,), 0, 4) == 0
    percent = jnp.repeat(jnp.where(crowded, 90, 15), LEAF_DEV)
    dice_rolls = jax.random.randint(jax.random.fold_in(key, 42), (LEAVES, REACH), 0, 100)
    leaf_index = jnp.arange(LEAVES, dtype=jnp.int32)[:, None]
    offsets = jnp.arange(1, REACH + 1, dtype=jnp.int32)[None, :]
    forward_pairs = (dice_rolls < percent[:, None]).astype(jnp.int32) * (leaf_index + offsets < LEAVES).astype(jnp.int32)
    behind = []
    for offset in range(REACH, 0, -1):
        moved = jnp.roll(forward_pairs[:, offset - 1], offset)
        behind.append(moved * (jnp.arange(LEAVES, dtype=jnp.int32) >= offset).astype(jnp.int32))
    middle = jnp.ones((LEAVES, 1), jnp.int32)
    return jnp.concatenate([jnp.stack(behind, axis=1), middle, forward_pairs], axis=1)


def draw_rhs(key, part):
    points = point_cloud(key)
    slopes = 0.15 * jax.random.normal(jax.random.fold_in(key, 51), (NRHS, DIM))
    phases = jax.random.uniform(jax.random.fold_in(key, 52), (NRHS, 1), minval=-3.1, maxval=3.1)
    smooth_wave = jnp.sin(jnp.dot(slopes, points, precision=lax.Precision.HIGHEST) + phases)
    rough_part = 0.3 * jnp.clip(jax.random.normal(jax.random.fold_in(key, 53), (NRHS, LEAVES * LEAF)), -3.0, 3.0)
    return smooth_wave + rough_part


def block_scale(key, shape, cuts, low, high):
    gain = 1.0
    for position, blocks in cuts:
        draws = jax.random.uniform(jax.random.fold_in(jax.random.fold_in(key, 6), position), (blocks,), jnp.float32, low / len(cuts), high / len(cuts))
        gain = gain * jnp.repeat(jnp.exp(draws), shape[position] // blocks).reshape((-1,) + (1,) * (len(shape) - 1 - position))
    return gain


def length_profile(number_of, total, bound, lean):
    portions = [(1 << 20) // math.isqrt(rank ** lean) + 1 for rank in range(2, number_of + 1)]
    spare, holding = total - bound - (number_of - 1), [1] * (number_of - 1)
    while spare > 0:
        free = [i for i in range(number_of - 1) if holding[i] < bound]
        mass, left = sum([portions[i] for i in free]), spare
        for i in free:
            addition = min(bound - holding[i], max(1, left * portions[i] // mass), spare)
            holding[i] = holding[i] + addition
            spare = spare - addition
    return np.array([bound] + holding)


def uneven(stream_key, count, total, limit, lean):
    if count == 2:
        one = jax.random.randint(stream_key, (), max(1, total - limit), min(limit, total - 1) + 1)
        return jnp.stack([one, total - one])
    tallies = jnp.asarray(length_profile(count, total, limit, lean), jnp.int32)
    pairs = (count - 1) // 2
    source_of, receiver = tallies[1:1 + 2 * pairs:2], tallies[2:2 + 2 * pairs:2]
    room = jnp.minimum(source_of - 1, limit - receiver)
    shifted = jax.random.randint(jax.random.fold_in(stream_key, 1), (pairs,), 0, 1 << 20) % (room + 1)
    tallies = tallies.at[1:1 + 2 * pairs:2].set(source_of - shifted).at[2:2 + 2 * pairs:2].set(receiver + shifted)
    return tallies[jax.random.permutation(jax.random.fold_in(stream_key, 2), count)]


def gaussian(stream_key, shape, deviation, reach, split=(), held_as=jnp.bfloat16):
    drawn = jax.random.normal(stream_key, shape, jnp.float32) * deviation
    if len(split) > 0:
        drawn = block_scale(stream_key, shape, split, -0.22, 0.18) * drawn
    return jnp.clip(drawn, min=-reach, max=reach).astype(held_as)


def setup_inputs(seed: int = 0) -> dict:
    key_of = jax.random.split(jax.random.key(seed), 9)
    coords = draw_coords(jax.random.fold_in(key_of[8], 71), 0)
    skeleton = draw_skeleton(jax.random.fold_in(key_of[8], 71), 0)
    transfer = gaussian(key_of[2], (LEAVES, RANK, RANK), RANK ** -0.5, 0.75, ((0, 8),))
    coupling = draw_coupling(jax.random.fold_in(key_of[8], 71), 0)
    parent = jnp.searchsorted(jnp.cumsum(uneven(key_of[4], LEVEL2, LEAVES, CHILD_MOST, 1)), jnp.arange(LEAVES), side="right").astype(jnp.int32)
    near_mask = draw_near_mask(jax.random.fold_in(key_of[8], 71), 0)
    noise = jnp.clip(jnp.exp(math.log(2.0) - 1.3862944 * jax.random.uniform(key_of[6], (POINTS,), jnp.float32) ** block_scale(key_of[6], (POINTS,), ((0, 8),), -0.2, 0.2)), 0.5, 2.0)
    rhs = draw_rhs(jax.random.fold_in(key_of[8], 71), 0)
    return {"coords": coords, "skeleton": skeleton, "transfer": transfer, "coupling": coupling, "parent": parent, "near_mask": near_mask, "noise": noise, "rhs": rhs}


HIGHEST = lax.Precision.HIGHEST
ROOT_THREE = 1.7320508075688772
LENGTH_SCALE = 4.0

def matern(row_coords, col_coords):
    cross = jnp.einsum('kdn,kdm->knm', row_coords, col_coords, precision=HIGHEST)
    first = lax.optimization_barrier(jnp.sum(row_coords * row_coords, axis=1))[:, :, None]
    second = lax.optimization_barrier(jnp.sum(col_coords * col_coords, axis=1))[:, None, :]
    scaled = ROOT_THREE / LENGTH_SCALE * jnp.sqrt(jnp.maximum(first + second - 2.0 * cross, 0.0))
    return (1.0 + scaled) * jnp.exp(-scaled)

def near_field(coords, values, near_mask):
    span_rows = REACH * LEAF
    col_width = (2 * REACH + 1) * LEAF
    padded_coords = jnp.pad(coords, ((0, 0), (span_rows, span_rows)))
    padded_values = jnp.pad(values, ((0, 0), (span_rows, span_rows)))

    def one_leaf(leaf_index):
        first_col = (leaf_index * LEAF).astype(jnp.int32)
        row_coords = lax.dynamic_slice_in_dim(coords, first_col, LEAF, 1)
        col_coords = lax.dynamic_slice_in_dim(padded_coords, first_col, col_width, 1)
        col_values = lax.dynamic_slice_in_dim(padded_values, first_col, col_width, 1)
        masking = jnp.repeat(near_mask[leaf_index].astype(jnp.float32), LEAF)
        kernel = matern(row_coords[None], col_coords[None])[0] * masking[None, :]
        return jnp.dot(col_values, kernel.T, precision=HIGHEST)
    blocks = lax.map(one_leaf, jnp.arange(LEAVES, dtype=jnp.int32))
    return jnp.transpose(blocks, (1, 0, 2)).reshape(NRHS, POINTS) / LEAF

def reference(coords, skeleton, transfer, coupling, parent, near_mask, noise, rhs):
    leaf_coords = jnp.transpose(coords.reshape(DIM, LEAVES, LEAF), (1, 0, 2))
    skeleton_coords = jnp.transpose(skeleton.reshape(DIM, LEAVES, RANK), (1, 0, 2))
    bases = matern(leaf_coords, skeleton_coords) / math.sqrt(LEAF)
    weights = transfer.astype(jnp.float32)
    coupled = coupling.astype(jnp.float32)
    members = (parent[:, None] == jnp.arange(LEVEL2, dtype=jnp.int32)[None, :]).astype(jnp.float32)
    counts = lax.optimization_barrier(jnp.sum(near_mask, axis=1)).astype(jnp.float32)
    diagonal = (noise.reshape(LEAVES, LEAF) + counts[:, None]).reshape(POINTS)

    def apply_operator(values):
        blocks = values.reshape(NRHS, LEAVES, LEAF)
        leaf_coeffs = jnp.einsum('cli,lir->lrc', blocks, bases, precision=HIGHEST)
        lifted = jnp.einsum('lrs,lrc->lsc', weights, leaf_coeffs, precision=HIGHEST)
        summed = jnp.einsum('lp,lsc->psc', members, lifted, precision=HIGHEST).reshape(LEVEL2 * RANK, NRHS)
        coupled_image = jnp.dot(coupled, summed, precision=HIGHEST)
        lowered = jnp.einsum('lp,psc->lsc', members, coupled_image.reshape(LEVEL2, RANK, NRHS), precision=HIGHEST)
        pushed = jnp.einsum('lrs,lsc->lrc', weights, lowered, precision=HIGHEST)
        far_part = jnp.einsum('lir,lrc->cli', bases, pushed, precision=HIGHEST).reshape(NRHS, POINTS)
        return diagonal[None, :] * values + near_field(coords, values, near_mask) + far_part
    solution = jnp.zeros_like(rhs)
    residual = rhs
    direction = rhs
    norm_now = lax.optimization_barrier(jnp.sum(residual * residual, axis=1))
    for iteration in range(ITERS):
        applied = apply_operator(direction)
        step_size = norm_now / lax.optimization_barrier(jnp.sum(direction * applied, axis=1))
        solution = solution + step_size[:, None] * direction
        residual = residual - step_size[:, None] * applied
        norm_next = lax.optimization_barrier(jnp.sum(residual * residual, axis=1))
        direction = residual + (norm_next / norm_now)[:, None] * direction
        norm_now = norm_next
    return (solution, residual)
```

```python
import functools
import math

import jax
import jax.numpy as jnp
from jax import lax
from jax.experimental import pallas as pl
from jax.experimental.pallas import tpu as pltpu
from jax.sharding import PartitionSpec as P

ITERS = 2
LENGTH_SCALE = 4.0
SCALE = math.sqrt(3.0) / LENGTH_SCALE
TILE = 256
KEEP_LOW = True
BF = jnp.bfloat16
F32 = jnp.float32
LANES = 128


def dot(a, b):
    return lax.dot_general(a, b, (((1,), (0,)), ((), ())), preferred_element_type=F32)


def dot_nt(a, b):
    return lax.dot_general(a, b, (((1,), (1,)), ((), ())), preferred_element_type=F32)


def split(x):
    high = x.astype(BF)
    return high, (x - high.astype(F32)).astype(BF)


def stacked(x):
    high = x.astype(BF).astype(F32)
    return jnp.concatenate([high, x - high], axis=0).astype(BF)


def folded(x):
    half = x.shape[0] // 2
    return x[:half] + x[half:]


def features(x):
    p = x * SCALE
    high = p.astype(BF).astype(F32)
    middle = (p - high).astype(BF).astype(F32)
    low = p - high - middle
    norm = jnp.sum(p * p, axis=0, keepdims=True)
    norm_high = norm.astype(BF).astype(F32)
    norm_middle = (norm - norm_high).astype(BF).astype(F32)
    norm_low = norm - norm_high - norm_middle
    row = lax.broadcasted_iota(jnp.int32, (8, x.shape[1]), 0)

    def norms(first):
        at = row - first
        return jnp.where(
            at == 0,
            norm_high,
            jnp.where(
                at == 1,
                norm_middle,
                jnp.where(at == 2, norm_low, jnp.where(row < 6, 1.0, 0.0)),
            ),
        )

    blank = jnp.zeros((8, x.shape[1]), F32)
    left = jnp.concatenate([high, middle, high, middle, low, high, norms(0), blank], axis=0)
    h2, m2, l2 = -2.0 * high, -2.0 * middle, -2.0 * low
    right = jnp.concatenate([h2, h2, m2, m2, h2, l2, norms(3), blank], axis=0)
    return left, right


def matern(left, right):
    squared = jnp.maximum(dot(left, right), 1e-30)
    s = squared * lax.rsqrt(squared)
    return (1.0 + s) * jnp.exp(-s)


def loop(count, body):
    if count <= 16:
        for i in range(count):
            body(i)
    else:
        lax.fori_loop(0, count, lambda i, c: (body(i), c)[1], 0)


def kernel(
    n,
    coords, skeleton, transfer, coupling, parent, near_mask, noise, rhs,
    solution_ref, residual_ref,
    halo_x, halo_v0, halo_v1, left_t, right_f, kept_high, kept_low,
    near_sum, moved, ut_high, ut_low, g_high, g_low,
    coef_out, coef_in, sum_out, sum_in,
    x_send, x_recv, v_send, v_recv, c_send, c_recv, i_send, i_recv,
):
    me = lax.axis_index("leaf")
    leaves, slots = near_mask.shape
    reach = slots // 2
    points = coords.shape[1]
    leaf = points // leaves
    rank = transfer.shape[1]
    wide = coupling.shape[0]
    count = rhs.shape[0]

    barrier = pltpu.get_barrier_semaphore()

    def greet(i):
        pl.semaphore_signal(
            barrier, inc=1, device_id={"leaf": lax.rem(me + i + 1, n)},
            device_id_type=pl.DeviceIdType.MESH,
        )

    loop(n - 1, greet)

    def copy(src, dst, send, recv, target):
        return pltpu.make_async_remote_copy(
            src_ref=src, dst_ref=dst, send_sem=send, recv_sem=recv,
            device_id={"leaf": target}, device_id_type=pl.DeviceIdType.MESH,
        )

    def halo(src, dst, send, recv):
        to_left = copy(src, dst.at[1], send.at[0], recv.at[1], jnp.maximum(me - 1, 0))
        to_right = copy(src, dst.at[0], send.at[1], recv.at[0], jnp.minimum(me + 1, n - 1))

        def start():
            pl.when(me > 0)(lambda: to_left.start())
            pl.when(me < n - 1)(lambda: to_right.start())

        def finish():
            @pl.when(me > 0)
            def _():
                to_left.wait_send()
                to_right.wait_recv()

            @pl.when(me < n - 1)
            def _():
                to_right.wait_send()
                to_left.wait_recv()

        return start, finish

    def spread(src, dst, send, recv):
        def one(i):
            return copy(src, dst.at[i], send.at[i], recv.at[i], lax.rem(me + i + 1, n))

        def start():
            loop(n - 1, lambda i: one(i).start())

        def finish():
            loop(n - 1, lambda i: one(i).wait())

        return start, finish

    def total(own, got):
        if n <= 16:
            value = own[...]
            for i in range(n - 1):
                value = value + got[i]
            return value
        return lax.fori_loop(0, n - 1, lambda i, s: s + got[i], own[...])

    @pl.when(me == 0)
    def _():
        for h in (halo_x, halo_v0, halo_v1):
            h[0] = jnp.zeros(h.shape[1:], F32)

    @pl.when(me == n - 1)
    def _():
        for h in (halo_x, halo_v0, halo_v1):
            h[1] = jnp.zeros(h.shape[1:], F32)

    pl.semaphore_wait(barrier, n - 1)
    start_x, finish_x = halo(coords, halo_x, x_send, x_recv)
    start_v, finish_v = halo(rhs, halo_v0, v_send.at[0], v_recv.at[0])
    start_x()
    start_v()

    left, right = features(coords[...])
    left_t[pl.ds(points, points)] = left.T.astype(BF)
    right_f[...] = right.astype(BF)

    skeleton_t = features(skeleton[...])[0].T.astype(BF)
    for l in range(leaves):
        across = pl.ds(l * leaf, leaf)
        bases_t = matern(skeleton_t[l * rank:(l + 1) * rank], right_f[:, across])
        b_high, b_low = split(bases_t * (1.0 / math.sqrt(leaf)))
        q = lax.broadcasted_iota(jnp.int32, (wide, rank), 0)
        s = lax.broadcasted_iota(jnp.int32, (wide, rank), 1)
        place = jnp.where(q == s + parent[l] * rank, 1.0, 0.0).astype(BF)
        placed = dot_nt(place, transfer[l]).astype(BF)
        ut = dot(placed, b_high) + dot(placed, b_low)
        u_high, u_low = split(ut)
        ut_high[:, across] = u_high
        ut_low[:, across] = u_low
        g = dot(coupling[...], u_high) + dot(coupling[...], u_low)
        g1, g2 = split(g)
        g_high[:, across] = g1
        g_low[:, across] = g2

    def far_up(v):
        both = stacked(v)
        return folded(dot_nt(both, ut_high[...])) + dot_nt(both[:count], ut_low[...])

    def far_down(s):
        both = stacked(s)
        image = folded(dot(both, coupling[...]))
        far = folded(dot(both, g_high[...])) + dot(both[:count], g_low[...])
        return image, far

    def row_sum(x):
        return jnp.sum(x, axis=1, keepdims=True)

    def send_coefs(it, v):
        coef_out[it, :, :wide] = far_up(v)
        coef_out[it, :, wide:] = jnp.broadcast_to(row_sum(v * v), (count, LANES))
        start, finish = spread(coef_out.at[it], coef_in.at[it], c_send.at[it], c_recv.at[it])
        start()
        return finish

    def near_block(l, t, first, columns):
        scale = near_mask[l, t].astype(F32) * (1.0 / leaf)
        across = slice(l * leaf, (l + 1) * leaf)
        acc = None
        for j in range(0, leaf, TILE):
            kept = pl.ds(t * leaf + j, TILE)
            if first:
                where = points + (l + t - reach) * leaf + j
                k = matern(left_t[where:where + TILE], right_f[:, across])
                k_high = k.astype(BF)
                kept_high[l, kept] = k_high
                if KEEP_LOW:
                    k_low = (k - k_high.astype(F32)).astype(BF)
                    kept_low[l, kept] = k_low
            else:
                k_high = kept_high[l, kept]
                if KEEP_LOW:
                    k_low = kept_low[l, kept]
            part = columns[:, j:j + TILE]
            term = folded(dot(part, k_high))
            if KEEP_LOW:
                term = term + dot(part[:count], k_low)
            acc = term if acc is None else acc + term
        near_sum[:, across] += scale * acc

    def near(first, v, halos, finish):
        near_sum[...] = jnp.zeros_like(near_sum)
        own = [], []
        for l in range(leaves):
            for t in range(slots):
                m = l + t - reach
                own[0 if 0 <= m < leaves else 1].append((l, t, m))
        both = stacked(v)
        for l, t, m in own[0]:
            near_block(l, t, first, both[:, m * leaf:(m + 1) * leaf])
        finish()
        if first:
            for side in range(2):
                far_left = features(halo_x[side])[0]
                left_t[pl.ds(2 * side * points, points)] = far_left.T.astype(BF)
        sides = [stacked(halos[0]), stacked(halos[1])]
        for l, t, m in own[1]:
            side = 0 if m < 0 else 1
            at = m + leaves if m < 0 else m - leaves
            near_block(l, t, first, sides[side][:, at * leaf:(at + 1) * leaf])
        diagonal = []
        for l in range(leaves):
            ones = near_mask[l, 0]
            for t in range(1, slots):
                ones = ones + near_mask[l, t]
            diagonal.append(noise[:, l * leaf:(l + 1) * leaf] + ones.astype(F32))
        return jnp.concatenate(diagonal, axis=1) * v + near_sum[...]

    def whole_pass(it, v, local, finish_c):
        sum_out[it] = jnp.broadcast_to(row_sum(v * local), (count, LANES))
        start, finish = spread(sum_out.at[it], sum_in.at[it], i_send.at[it], i_recv.at[it])
        start()
        finish_c()
        value = total(coef_out.at[it], coef_in.at[it])
        s, norm = value[:, :wide], value[:, wide:wide + 1]
        image, far = far_down(s)
        extra = row_sum(s * image)
        finish()
        inner = total(sum_out.at[it], sum_in.at[it])[:, :1] + extra
        return local + far, norm, inner

    r0 = rhs[...]
    finish_c = send_coefs(0, r0)

    def arrived():
        finish_x()
        finish_v()

    local = near(True, r0, halo_v0, arrived)
    applied0, norm0, inner0 = whole_pass(0, r0, local, finish_c)
    step0 = norm0 / inner0
    r1 = r0 - step0 * applied0
    moved[...] = r1
    solution_ref[...] = step0 * r0
    residual_ref[...] = applied0
    start_v, finish_v1 = halo(moved, halo_v1, v_send.at[1], v_recv.at[1])
    start_v()

    finish_c = send_coefs(1, r1)
    local = near(False, r1, halo_v1, finish_v1)
    applied1, norm1, inner1 = whole_pass(1, r1, local, finish_c)
    growth = norm1 / norm0
    step1 = norm1 / (inner1 - growth * norm1 / step0)
    solution_ref[...] = solution_ref[...] + step1 * (r1 + growth * rhs[...])
    residual_ref[...] = r1 - step1 * (applied1 + growth * residual_ref[...])


def per_device(coords, skeleton, transfer, coupling, parent, near_mask, noise, rhs):
    n = lax.axis_size("leaf")
    leaves, slots = near_mask.shape
    points = coords.shape[1]
    leaf = points // leaves
    wide = coupling.shape[0]
    count = rhs.shape[0]
    vmem = pl.BlockSpec(memory_space=pltpu.VMEM)
    smem = pl.BlockSpec(memory_space=pltpu.SMEM)
    peers = max(n - 1, 1)
    dma = pltpu.SemaphoreType.DMA
    return pl.pallas_call(
        functools.partial(kernel, n),
        out_shape=(jax.ShapeDtypeStruct(rhs.shape, F32),) * 2,
        in_specs=[vmem, vmem, vmem, vmem, smem, smem, vmem, vmem],
        out_specs=(vmem, vmem),
        scratch_shapes=[
            pltpu.VMEM((2,) + coords.shape, F32),
            pltpu.VMEM((2, count, points), F32),
            pltpu.VMEM((2, count, points), F32),
            pltpu.VMEM((3 * points, 64), BF),
            pltpu.VMEM((64, points), BF),
            pltpu.VMEM((leaves, slots * leaf, leaf), BF),
            pltpu.VMEM((leaves, slots * leaf, leaf) if KEEP_LOW else (1, 16, LANES), BF),
            pltpu.VMEM((count, points), F32),
            pltpu.VMEM((count, points), F32),
            pltpu.VMEM((wide, points), BF),
            pltpu.VMEM((wide, points), BF),
            pltpu.VMEM((wide, points), BF),
            pltpu.VMEM((wide, points), BF),
            pltpu.VMEM((ITERS, count, wide + LANES), F32),
            pltpu.VMEM((ITERS, peers, count, wide + LANES), F32),
            pltpu.VMEM((ITERS, count, LANES), F32),
            pltpu.VMEM((ITERS, peers, count, LANES), F32),
            dma((2,)), dma((2,)), dma((2, 2)), dma((2, 2)),
            dma((ITERS, peers)), dma((ITERS, peers)), dma((ITERS, peers)), dma((ITERS, peers)),
        ],
        compiler_params=pltpu.CompilerParams(
            collective_id=0, has_side_effects=True, vmem_limit_bytes=60 * 1024 * 1024
        ),
    )(coords, skeleton, transfer, coupling, parent, near_mask, noise.reshape(1, points), rhs)


def solution(mesh):
    return jax.shard_map(
        per_device,
        mesh=mesh,
        in_specs=(
            P(None, "leaf"),
            P(None, "leaf"),
            P("leaf", None, None),
            P(),
            P("leaf"),
            P("leaf", None),
            P("leaf"),
            P("rep", "leaf"),
        ),
        out_specs=(P("rep", "leaf"), P("rep", "leaf")),
        check_vma=False,
    )
```

```python
import functools
import math

import jax
import jax.numpy as jnp
from jax import lax
from jax.experimental import pallas as pl
from jax.experimental.pallas import tpu as pltpu
from jax.sharding import PartitionSpec as P

ITERS = 2
LENGTH_SCALE = 4.0
SCALE = math.sqrt(3.0) / LENGTH_SCALE
TILE = 256
KEEP_LOW = True
BF = jnp.bfloat16
F32 = jnp.float32
LANES = 128


def dot(a, b):
    return lax.dot_general(a, b, (((1,), (0,)), ((), ())), preferred_element_type=F32)


def dot_nt(a, b):
    return lax.dot_general(a, b, (((1,), (1,)), ((), ())), preferred_element_type=F32)


def split(x):
    high = x.astype(BF)
    return high, (x - high.astype(F32)).astype(BF)


def stacked(x):
    high = x.astype(BF).astype(F32)
    return jnp.concatenate([high, x - high], axis=0).astype(BF)


def folded(x):
    half = x.shape[0] // 2
    return x[:half] + x[half:]


def features(x):
    p = x * SCALE
    high = p.astype(BF).astype(F32)
    middle = (p - high).astype(BF).astype(F32)
    low = p - high - middle
    norm = jnp.sum(p * p, axis=0, keepdims=True)
    norm_high = norm.astype(BF).astype(F32)
    norm_middle = (norm - norm_high).astype(BF).astype(F32)
    norm_low = norm - norm_high - norm_middle
    row = lax.broadcasted_iota(jnp.int32, (8, x.shape[1]), 0)

    def norms(first):
        at = row - first
        return jnp.where(
            at == 0,
            norm_high,
            jnp.where(
                at == 1,
                norm_middle,
                jnp.where(at == 2, norm_low, jnp.where(row < 6, 1.0, 0.0)),
            ),
        )

    blank = jnp.zeros((8, x.shape[1]), F32)
    left = jnp.concatenate([high, middle, high, middle, low, high, norms(0), blank], axis=0)
    h2, m2, l2 = -2.0 * high, -2.0 * middle, -2.0 * low
    right = jnp.concatenate([h2, h2, m2, m2, h2, l2, norms(3), blank], axis=0)
    return left, right


def matern(left, right):
    squared = jnp.maximum(dot(left, right), 1e-30)
    s = squared * lax.rsqrt(squared)
    return (1.0 + s) * jnp.exp(-s)


def loop(count, body):
    if count <= 16:
        for i in range(count):
            body(i)
    else:
        lax.fori_loop(0, count, lambda i, c: (body(i), c)[1], 0)


def kernel(
    n,
    coords, skeleton, transfer, coupling, parent, near_mask, noise, rhs,
    solution_ref, residual_ref,
    halo_x, halo_v0, halo_v1, left_t, right_f, kept_high, kept_low,
    near_sum, moved, ut_high, ut_low, g_high, g_low,
    coef_out, coef_in, sum_out, sum_in,
    x_send, x_recv, v_send, v_recv, c_send, c_recv, i_send, i_recv, ready,
):
    me = lax.axis_index("leaf")
    leaves, slots = near_mask.shape
    reach = slots // 2
    points = coords.shape[1]
    leaf = points // leaves
    rank = transfer.shape[1]
    wide = coupling.shape[0]
    count = rhs.shape[0]

    barrier = pltpu.get_barrier_semaphore()

    def tell(sem, target):
        pl.semaphore_signal(
            sem, inc=1, device_id={"leaf": target}, device_id_type=pl.DeviceIdType.MESH
        )

    stages = n.bit_length() - 1
    partners = [me + 2**b * (1 - 2 * lax.rem(me // 2**b, 2)) for b in range(stages)]
    other = me - 1 + 2 * lax.rem(me, 2)
    has_other = jnp.logical_and(other >= 0, other < n)
    for target in partners:
        tell(barrier, target)
    pl.when(has_other)(lambda: tell(barrier, other))

    def stage(b):
        def run():
            if b > 0:
                pl.semaphore_wait(ready.at[b - 1], 1)
            if b < stages:
                tell(ready.at[b], partners[b])
        return run

    def copy(src, dst, send, recv, target):
        return pltpu.make_async_remote_copy(
            src_ref=src, dst_ref=dst, send_sem=send, recv_sem=recv,
            device_id={"leaf": target}, device_id_type=pl.DeviceIdType.MESH,
        )

    def halo(src, dst, send, recv):
        to_left = copy(src, dst.at[1], send.at[0], recv.at[1], jnp.maximum(me - 1, 0))
        to_right = copy(src, dst.at[0], send.at[1], recv.at[0], jnp.minimum(me + 1, n - 1))

        def start():
            pl.when(me > 0)(lambda: to_left.start())
            pl.when(me < n - 1)(lambda: to_right.start())

        def finish():
            @pl.when(me > 0)
            def _():
                to_left.wait_send()
                to_right.wait_recv()

            @pl.when(me < n - 1)
            def _():
                to_right.wait_send()
                to_left.wait_recv()

        return start, finish

    def spread(src, dst, send, recv):
        def one(i):
            return copy(src, dst.at[i], send.at[i], recv.at[i], lax.rem(me + i + 1, n))

        def start():
            loop(n - 1, lambda i: one(i).start())

        def finish():
            loop(n - 1, lambda i: one(i).wait())

        return start, finish

    def total(own, got):
        if n <= 16:
            value = own[...]
            for i in range(n - 1):
                value = value + got[i]
            return value
        return lax.fori_loop(0, n - 1, lambda i, s: s + got[i], own[...])

    @pl.when(me == 0)
    def _():
        for h in (halo_x, halo_v0, halo_v1):
            h[0] = jnp.zeros(h.shape[1:], F32)

    @pl.when(me == n - 1)
    def _():
        for h in (halo_x, halo_v0, halo_v1):
            h[1] = jnp.zeros(h.shape[1:], F32)

    pl.when(has_other)(lambda: pl.semaphore_wait(barrier, stages + 1))
    pl.when(jnp.logical_not(has_other))(lambda: pl.semaphore_wait(barrier, stages))
    stage(0)()
    start_x, finish_x = halo(coords, halo_x, x_send, x_recv)
    start_v, finish_v = halo(rhs, halo_v0, v_send.at[0], v_recv.at[0])
    start_x()
    start_v()

    left, right = features(coords[...])
    left_t[pl.ds(points, points)] = left.T.astype(BF)
    right_f[...] = right.astype(BF)

    skeleton_t = features(skeleton[...])[0].T.astype(BF)
    for l in range(leaves):
        across = pl.ds(l * leaf, leaf)
        bases_t = matern(skeleton_t[l * rank:(l + 1) * rank], right_f[:, across])
        b_high, b_low = split(bases_t * (1.0 / math.sqrt(leaf)))
        q = lax.broadcasted_iota(jnp.int32, (wide, rank), 0)
        s = lax.broadcasted_iota(jnp.int32, (wide, rank), 1)
        place = jnp.where(q == s + parent[l] * rank, 1.0, 0.0).astype(BF)
        placed = dot_nt(place, transfer[l]).astype(BF)
        ut = dot(placed, b_high) + dot(placed, b_low)
        u_high, u_low = split(ut)
        ut_high[:, across] = u_high
        ut_low[:, across] = u_low
        g = dot(coupling[...], u_high) + dot(coupling[...], u_low)
        g1, g2 = split(g)
        g_high[:, across] = g1
        g_low[:, across] = g2

    def far_up(v):
        both = stacked(v)
        return folded(dot_nt(both, ut_high[...])) + dot_nt(both[:count], ut_low[...])

    def far_down(s):
        both = stacked(s)
        image = folded(dot(both, coupling[...]))
        far = folded(dot(both, g_high[...])) + dot(both[:count], g_low[...])
        return image, far

    lane = lax.broadcasted_iota(jnp.int32, (count, LANES), 1)
    on_diagonal = lane == lax.broadcasted_iota(jnp.int32, (count, LANES), 0)

    def to_row(x):
        return jnp.sum(jnp.where(on_diagonal, x, 0.0), axis=0, keepdims=True)

    def to_col(x):
        return jnp.sum(jnp.where(on_diagonal, x, 0.0), axis=1, keepdims=True)

    def row_sum(x):
        return jnp.sum(x, axis=1, keepdims=True)

    def send_coefs(it, v):
        coef_out[it] = far_up(v)
        return spread(coef_out.at[it], coef_in.at[it], c_send.at[it], c_recv.at[it])

    def near_block(l, t, first, columns):
        scale = near_mask[l, t].astype(F32) * (1.0 / leaf)
        across = slice(l * leaf, (l + 1) * leaf)
        acc = None
        for j in range(0, leaf, TILE):
            kept = pl.ds(t * leaf + j, TILE)
            if first:
                where = points + (l + t - reach) * leaf + j
                k = matern(left_t[where:where + TILE], right_f[:, across])
                k_high = k.astype(BF)
                kept_high[l, kept] = k_high
                if KEEP_LOW:
                    k_low = (k - k_high.astype(F32)).astype(BF)
                    kept_low[l, kept] = k_low
            else:
                k_high = kept_high[l, kept]
                if KEEP_LOW:
                    k_low = kept_low[l, kept]
            part = columns[:, j:j + TILE]
            term = folded(dot(part, k_high))
            if KEEP_LOW:
                term = term + dot(part[:count], k_low)
            acc = term if acc is None else acc + term
        near_sum[:, across] += scale * acc

    def near(first, v, halos, finish, between):
        near_sum[...] = jnp.zeros_like(near_sum)
        own = [], []
        for l in range(leaves):
            for t in range(slots):
                m = l + t - reach
                own[0 if 0 <= m < leaves else 1].append((l, t, m))
        both = stacked(v)
        for l, t, m in own[0]:
            near_block(l, t, first, both[:, m * leaf:(m + 1) * leaf])
            if between:
                between.pop(0)()
        for step in between:
            step()
        finish()
        if first:
            for side in range(2):
                far_left = features(halo_x[side])[0]
                left_t[pl.ds(2 * side * points, points)] = far_left.T.astype(BF)
        sides = [stacked(halos[0]), stacked(halos[1])]
        for l, t, m in own[1]:
            side = 0 if m < 0 else 1
            at = m + leaves if m < 0 else m - leaves
            near_block(l, t, first, sides[side][:, at * leaf:(at + 1) * leaf])
        diagonal = []
        for l in range(leaves):
            ones = near_mask[l, 0]
            for t in range(1, slots):
                ones = ones + near_mask[l, t]
            diagonal.append(noise[:, l * leaf:(l + 1) * leaf] + ones.astype(F32))
        return jnp.concatenate(diagonal, axis=1) * v + near_sum[...]

    def whole_pass(it, v, local, finish_c):
        sum_out[it, :1] = to_row(row_sum(v * local))
        sum_out[it, 1:] = to_row(row_sum(v * v))
        start, finish = spread(sum_out.at[it], sum_in.at[it], i_send.at[it], i_recv.at[it])
        start()
        finish_c()
        s = total(coef_out.at[it], coef_in.at[it])
        image, far = far_down(s)
        extra = row_sum(s * image)
        finish()
        sums = total(sum_out.at[it], sum_in.at[it])
        return local + far, to_col(sums[1:]), to_col(sums[:1]) + extra

    r0 = rhs[...]
    start_c, finish_c = send_coefs(0, r0)

    def arrived():
        finish_x()
        finish_v()

    between = [stage(b) for b in range(1, stages + 1)] + [start_c]
    local = near(True, r0, halo_v0, arrived, between)
    applied0, norm0, inner0 = whole_pass(0, r0, local, finish_c)
    step0 = norm0 / inner0
    r1 = r0 - step0 * applied0
    moved[...] = r1
    solution_ref[...] = step0 * r0
    residual_ref[...] = applied0
    start_v, finish_v1 = halo(moved, halo_v1, v_send.at[1], v_recv.at[1])
    start_v()

    start_c, finish_c = send_coefs(1, r1)
    start_c()
    local = near(False, r1, halo_v1, finish_v1, [])
    applied1, norm1, inner1 = whole_pass(1, r1, local, finish_c)
    growth = norm1 / norm0
    step1 = norm1 / (inner1 - growth * norm1 / step0)
    solution_ref[...] = solution_ref[...] + step1 * (r1 + growth * rhs[...])
    residual_ref[...] = r1 - step1 * (applied1 + growth * residual_ref[...])


def per_device(coords, skeleton, transfer, coupling, parent, near_mask, noise, rhs):
    n = lax.axis_size("leaf")
    leaves, slots = near_mask.shape
    points = coords.shape[1]
    leaf = points // leaves
    wide = coupling.shape[0]
    count = rhs.shape[0]
    vmem = pl.BlockSpec(memory_space=pltpu.VMEM)
    smem = pl.BlockSpec(memory_space=pltpu.SMEM)
    peers = max(n - 1, 1)
    dma = pltpu.SemaphoreType.DMA
    return pl.pallas_call(
        functools.partial(kernel, n),
        out_shape=(jax.ShapeDtypeStruct(rhs.shape, F32),) * 2,
        in_specs=[vmem, vmem, vmem, vmem, smem, smem, vmem, vmem],
        out_specs=(vmem, vmem),
        scratch_shapes=[
            pltpu.VMEM((2,) + coords.shape, F32),
            pltpu.VMEM((2, count, points), F32),
            pltpu.VMEM((2, count, points), F32),
            pltpu.VMEM((3 * points, 64), BF),
            pltpu.VMEM((64, points), BF),
            pltpu.VMEM((leaves, slots * leaf, leaf), BF),
            pltpu.VMEM((leaves, slots * leaf, leaf) if KEEP_LOW else (1, 16, LANES), BF),
            pltpu.VMEM((count, points), F32),
            pltpu.VMEM((count, points), F32),
            pltpu.VMEM((wide, points), BF),
            pltpu.VMEM((wide, points), BF),
            pltpu.VMEM((wide, points), BF),
            pltpu.VMEM((wide, points), BF),
            pltpu.VMEM((ITERS, count, wide), F32),
            pltpu.VMEM((ITERS, peers, count, wide), F32),
            pltpu.VMEM((ITERS, 2, LANES), F32),
            pltpu.VMEM((ITERS, peers, 2, LANES), F32),
            dma((2,)), dma((2,)), dma((2, 2)), dma((2, 2)),
            dma((ITERS, peers)), dma((ITERS, peers)), dma((ITERS, peers)), dma((ITERS, peers)),
            pltpu.SemaphoreType.REGULAR((max(n.bit_length() - 1, 1),)),
        ],
        compiler_params=pltpu.CompilerParams(
            collective_id=0, has_side_effects=True, vmem_limit_bytes=60 * 1024 * 1024
        ),
    )(coords, skeleton, transfer, coupling, parent, near_mask, noise.reshape(1, points), rhs)


def solution(mesh):
    return jax.shard_map(
        per_device,
        mesh=mesh,
        in_specs=(
            P(None, "leaf"),
            P(None, "leaf"),
            P("leaf", None, None),
            P(),
            P("leaf"),
            P("leaf", None),
            P("leaf"),
            P("rep", "leaf"),
        ),
        out_specs=(P("rep", "leaf"), P("rep", "leaf")),
        check_vma=False,
    )
```

```python
import functools
import math

import jax
import jax.numpy as jnp
from jax import lax
from jax.experimental import pallas as pl
from jax.experimental.pallas import tpu as pltpu
from jax.sharding import PartitionSpec as P

ITERS = 2
LENGTH_SCALE = 4.0
SCALE = math.sqrt(3.0) / LENGTH_SCALE
TILE = 256
KEEP_LOW = True
BF = jnp.bfloat16
F32 = jnp.float32
LANES = 128


def dot(a, b):
    return lax.dot_general(a, b, (((1,), (0,)), ((), ())), preferred_element_type=F32)


def dot_nt(a, b):
    return lax.dot_general(a, b, (((1,), (1,)), ((), ())), preferred_element_type=F32)


def split(x):
    high = x.astype(BF)
    return high, (x - high.astype(F32)).astype(BF)


def stacked(x):
    high = x.astype(BF).astype(F32)
    return jnp.concatenate([high, x - high], axis=0).astype(BF)


def folded(x):
    half = x.shape[0] // 2
    return x[:half] + x[half:]


def features(x):
    p = x * SCALE
    high = p.astype(BF).astype(F32)
    middle = (p - high).astype(BF).astype(F32)
    low = p - high - middle
    norm = jnp.sum(p * p, axis=0, keepdims=True)
    norm_high = norm.astype(BF).astype(F32)
    norm_middle = (norm - norm_high).astype(BF).astype(F32)
    norm_low = norm - norm_high - norm_middle
    row = lax.broadcasted_iota(jnp.int32, (8, x.shape[1]), 0)

    def norms(first):
        at = row - first
        return jnp.where(
            at == 0,
            norm_high,
            jnp.where(
                at == 1,
                norm_middle,
                jnp.where(at == 2, norm_low, jnp.where(row < 6, 1.0, 0.0)),
            ),
        )

    blank = jnp.zeros((8, x.shape[1]), F32)
    left = jnp.concatenate([high, middle, high, middle, low, high, norms(0), blank], axis=0)
    h2, m2, l2 = -2.0 * high, -2.0 * middle, -2.0 * low
    right = jnp.concatenate([h2, h2, m2, m2, h2, l2, norms(3), blank], axis=0)
    return left, right


def matern(left, right):
    squared = jnp.maximum(dot(left, right), 1e-30)
    s = squared * lax.rsqrt(squared)
    return (1.0 + s) * jnp.exp(-s)


def loop(count, body):
    if count <= 16:
        for i in range(count):
            body(i)
    else:
        lax.fori_loop(0, count, lambda i, c: (body(i), c)[1], 0)


def kernel(
    n,
    coords, skeleton, transfer, coupling, parent, near_mask, noise, rhs,
    solution_ref, residual_ref,
    halo_x, halo_v0, halo_v1, left_t, right_f, kept_high, kept_low,
    near_sum, moved, ut_high, ut_low, g_high, g_low,
    coef_out, coef_in, sum_out, sum_in,
    x_send, x_recv, v_send, v_recv, c_send, c_recv, i_send, i_recv, ready,
    halo_s, halo_t, halo_p, own_t, own_p, gh_high, gh_low, e_send, e_recv,
):
    me = lax.axis_index("leaf")
    leaves, slots = near_mask.shape
    reach = slots // 2
    points = coords.shape[1]
    leaf = points // leaves
    rank = transfer.shape[1]
    wide = coupling.shape[0]
    count = rhs.shape[0]

    barrier = pltpu.get_barrier_semaphore()

    def tell(sem, target):
        pl.semaphore_signal(
            sem, inc=1, device_id={"leaf": target}, device_id_type=pl.DeviceIdType.MESH
        )

    stages = n.bit_length() - 1
    partners = [me + 2**b * (1 - 2 * lax.rem(me // 2**b, 2)) for b in range(stages)]
    other = me - 1 + 2 * lax.rem(me, 2)
    has_other = jnp.logical_and(other >= 0, other < n)
    for target in partners:
        tell(barrier, target)
    pl.when(has_other)(lambda: tell(barrier, other))

    def stage(b):
        def run():
            if b > 0:
                pl.semaphore_wait(ready.at[b - 1], 1)
            if b < stages:
                tell(ready.at[b], partners[b])
        return run

    def copy(src, dst, send, recv, target):
        return pltpu.make_async_remote_copy(
            src_ref=src, dst_ref=dst, send_sem=send, recv_sem=recv,
            device_id={"leaf": target}, device_id_type=pl.DeviceIdType.MESH,
        )

    def halo(src, dst, send, recv):
        to_left = copy(src, dst.at[1], send.at[0], recv.at[1], jnp.maximum(me - 1, 0))
        to_right = copy(src, dst.at[0], send.at[1], recv.at[0], jnp.minimum(me + 1, n - 1))

        def start():
            pl.when(me > 0)(lambda: to_left.start())
            pl.when(me < n - 1)(lambda: to_right.start())

        def finish():
            @pl.when(me > 0)
            def _():
                to_left.wait_send()
                to_right.wait_recv()

            @pl.when(me < n - 1)
            def _():
                to_right.wait_send()
                to_left.wait_recv()

        return start, finish

    def spread(src, dst, send, recv):
        def one(i):
            return copy(src, dst.at[i], send.at[i], recv.at[i], lax.rem(me + i + 1, n))

        def start():
            loop(n - 1, lambda i: one(i).start())

        def finish():
            loop(n - 1, lambda i: one(i).wait())

        return start, finish

    def total(own, got):
        if n <= 16:
            value = own[...]
            for i in range(n - 1):
                value = value + got[i]
            return value
        return lax.fori_loop(0, n - 1, lambda i, s: s + got[i], own[...])

    @pl.when(me == 0)
    def _():
        for h in (halo_x, halo_v0, halo_v1, halo_s, halo_t, halo_p):
            h[0] = jnp.zeros(h.shape[1:], F32)

    @pl.when(me == n - 1)
    def _():
        for h in (halo_x, halo_v0, halo_v1, halo_s, halo_t, halo_p):
            h[1] = jnp.zeros(h.shape[1:], F32)

    own_t[...] = transfer[...].astype(F32)
    parent_row = lax.broadcasted_iota(jnp.int32, (8, LANES), 0)
    parents = jnp.zeros((8, LANES), F32)
    for l in range(leaves):
        parents = jnp.where(parent_row == l, parent[l].astype(F32), parents)
    own_p[...] = parents
    pl.when(has_other)(lambda: pl.semaphore_wait(barrier, stages + 1))
    pl.when(jnp.logical_not(has_other))(lambda: pl.semaphore_wait(barrier, stages))
    stage(0)()
    start_x, finish_x = halo(coords, halo_x, x_send, x_recv)
    start_v, finish_v = halo(rhs, halo_v0, v_send.at[0], v_recv.at[0])
    start_x()
    start_v()
    extras = [
        halo(a, b, e_send.at[i], e_recv.at[i])
        for i, (a, b) in enumerate(((skeleton, halo_s), (own_t, halo_t), (own_p, halo_p)))
    ]
    for start, _ in extras:
        start()

    left, right = features(coords[...])
    left_t[pl.ds(points, points)] = left.T.astype(BF)
    right_f[...] = right.astype(BF)

    skeleton_t = features(skeleton[...])[0].T.astype(BF)
    q = lax.broadcasted_iota(jnp.int32, (wide, rank), 0)
    q = (q - lax.broadcasted_iota(jnp.int32, (wide, rank), 1)).astype(F32)

    def upward(skel, right, where, weights):
        bases_t = matern(skel, right)
        b_high, b_low = split(bases_t * (1.0 / math.sqrt(leaf)))
        place = jnp.where(q == where * rank, 1.0, 0.0).astype(BF)
        placed = dot_nt(place, weights).astype(BF)
        return split(dot(placed, b_high) + dot(placed, b_low))

    for l in range(leaves):
        across = pl.ds(l * leaf, leaf)
        u_high, u_low = upward(
            skeleton_t[l * rank:(l + 1) * rank], right_f[:, across],
            parent[l].astype(F32), transfer[l],
        )
        ut_high[:, across] = u_high
        ut_low[:, across] = u_low
        g = dot(coupling[...], u_high) + dot(coupling[...], u_low)
        g1, g2 = split(g)
        g_high[:, across] = g1
        g_low[:, across] = g2

    def couple_halo():
        for _, finish in extras:
            finish()
        for side in range(2):
            right = features(halo_x[side])[1].astype(BF)
            skel = features(halo_s[side])[0].T.astype(BF)
            for l in range(leaves):
                across = slice(l * leaf, (l + 1) * leaf)
                u_high, u_low = upward(
                    skel[l * rank:(l + 1) * rank], right[:, across],
                    halo_p[side, l:l + 1, :1], halo_t[side, l].astype(BF),
                )
                g1, g2 = split(dot(coupling[...], u_high) + dot(coupling[...], u_low))
                gh_high[side, :, across] = g1
                gh_low[side, :, across] = g2

    def far_up(v):
        both = stacked(v)
        return folded(dot_nt(both, ut_high[...])) + dot_nt(both[:count], ut_low[...])

    def far_down(s):
        both = stacked(s)
        image = folded(dot(both, coupling[...]))
        far = folded(dot(both, g_high[...])) + dot(both[:count], g_low[...])
        return image, far

    lane = lax.broadcasted_iota(jnp.int32, (count, LANES), 1)
    on_diagonal = lane == lax.broadcasted_iota(jnp.int32, (count, LANES), 0)

    def to_row(x):
        return jnp.sum(jnp.where(on_diagonal, x, 0.0), axis=0, keepdims=True)

    def to_col(x):
        return jnp.sum(jnp.where(on_diagonal, x, 0.0), axis=1, keepdims=True)

    def row_sum(x):
        return jnp.sum(x, axis=1, keepdims=True)

    def send_coefs(it, v):
        coef_out[it] = far_up(v)
        return spread(coef_out.at[it], coef_in.at[it], c_send.at[it], c_recv.at[it])

    def near_block(l, t, first, columns):
        scale = near_mask[l, t].astype(F32) * (1.0 / leaf)
        across = slice(l * leaf, (l + 1) * leaf)
        acc = None
        for j in range(0, leaf, TILE):
            kept = pl.ds(t * leaf + j, TILE)
            if first:
                where = points + (l + t - reach) * leaf + j
                k = matern(left_t[where:where + TILE], right_f[:, across])
                k_high = k.astype(BF)
                kept_high[l, kept] = k_high
                if KEEP_LOW:
                    k_low = (k - k_high.astype(F32)).astype(BF)
                    kept_low[l, kept] = k_low
            else:
                k_high = kept_high[l, kept]
                if KEEP_LOW:
                    k_low = kept_low[l, kept]
            part = columns[:, j:j + TILE]
            term = folded(dot(part, k_high))
            if KEEP_LOW:
                term = term + dot(part[:count], k_low)
            acc = term if acc is None else acc + term
        near_sum[:, across] += scale * acc

    def near(first, v, halos, finish, between):
        near_sum[...] = jnp.zeros_like(near_sum)
        own = [], []
        for l in range(leaves):
            for t in range(slots):
                m = l + t - reach
                own[0 if 0 <= m < leaves else 1].append((l, t, m))
        both = stacked(v)
        for l, t, m in own[0]:
            near_block(l, t, first, both[:, m * leaf:(m + 1) * leaf])
            if between:
                between.pop(0)()
        for step in between:
            step()
        finish()
        if first:
            for side in range(2):
                far_left = features(halo_x[side])[0]
                left_t[pl.ds(2 * side * points, points)] = far_left.T.astype(BF)
        sides = [stacked(halos[0]), stacked(halos[1])]
        for l, t, m in own[1]:
            side = 0 if m < 0 else 1
            at = m + leaves if m < 0 else m - leaves
            near_block(l, t, first, sides[side][:, at * leaf:(at + 1) * leaf])
        diagonal = []
        for l in range(leaves):
            ones = near_mask[l, 0]
            for t in range(1, slots):
                ones = ones + near_mask[l, t]
            diagonal.append(noise[:, l * leaf:(l + 1) * leaf] + ones.astype(F32))
        return jnp.concatenate(diagonal, axis=1) * v + near_sum[...]

    def whole_pass(it, v, local, finish_c, during):
        sum_out[it, :1] = to_row(row_sum(v * local))
        sum_out[it, 1:] = to_row(row_sum(v * v))
        start, finish = spread(sum_out.at[it], sum_in.at[it], i_send.at[it], i_recv.at[it])
        start()
        during()
        finish_c()
        s = total(coef_out.at[it], coef_in.at[it])
        image, far = far_down(s)
        extra = row_sum(s * image)
        finish()
        sums = total(sum_out.at[it], sum_in.at[it])
        return local + far, to_col(sums[1:]), to_col(sums[:1]) + extra, s

    r0 = rhs[...]
    start_c, finish_c = send_coefs(0, r0)

    def arrived():
        finish_x()
        finish_v()

    between = [stage(b) for b in range(1, stages + 1)] + [start_c]
    local = near(True, r0, halo_v0, arrived, between)
    moved[...] = local
    start_v, finish_v1 = halo(moved, halo_v1, v_send.at[1], v_recv.at[1])

    def during():
        start_v()
        couple_halo()

    applied0, norm0, inner0, s0 = whole_pass(0, r0, local, finish_c, during)
    step0 = norm0 / inner0
    r1 = r0 - step0 * applied0
    solution_ref[...] = step0 * r0
    residual_ref[...] = applied0

    start_c, finish_c = send_coefs(1, r1)
    start_c()

    finish_v1()
    both0 = stacked(s0)
    moved_in = []
    for side in range(2):
        far = folded(dot(both0, gh_high[side])) + dot(both0[:count], gh_low[side])
        moved_in.append(halo_v0[side] - step0 * (halo_v1[side] + far))
    local = near(False, r1, moved_in, lambda: None, [])
    applied1, norm1, inner1, _ = whole_pass(1, r1, local, finish_c, lambda: None)
    growth = norm1 / norm0
    step1 = norm1 / (inner1 - growth * norm1 / step0)
    solution_ref[...] = solution_ref[...] + step1 * (r1 + growth * rhs[...])
    residual_ref[...] = r1 - step1 * (applied1 + growth * residual_ref[...])


def per_device(coords, skeleton, transfer, coupling, parent, near_mask, noise, rhs):
    n = lax.axis_size("leaf")
    leaves, slots = near_mask.shape
    points = coords.shape[1]
    leaf = points // leaves
    wide = coupling.shape[0]
    count = rhs.shape[0]
    vmem = pl.BlockSpec(memory_space=pltpu.VMEM)
    smem = pl.BlockSpec(memory_space=pltpu.SMEM)
    peers = max(n - 1, 1)
    dma = pltpu.SemaphoreType.DMA
    return pl.pallas_call(
        functools.partial(kernel, n),
        out_shape=(jax.ShapeDtypeStruct(rhs.shape, F32),) * 2,
        in_specs=[vmem, vmem, vmem, vmem, smem, smem, vmem, vmem],
        out_specs=(vmem, vmem),
        scratch_shapes=[
            pltpu.VMEM((2,) + coords.shape, F32),
            pltpu.VMEM((2, count, points), F32),
            pltpu.VMEM((2, count, points), F32),
            pltpu.VMEM((3 * points, 64), BF),
            pltpu.VMEM((64, points), BF),
            pltpu.VMEM((leaves, slots * leaf, leaf), BF),
            pltpu.VMEM((leaves, slots * leaf, leaf) if KEEP_LOW else (1, 16, LANES), BF),
            pltpu.VMEM((count, points), F32),
            pltpu.VMEM((count, points), F32),
            pltpu.VMEM((wide, points), BF),
            pltpu.VMEM((wide, points), BF),
            pltpu.VMEM((wide, points), BF),
            pltpu.VMEM((wide, points), BF),
            pltpu.VMEM((ITERS, count, wide), F32),
            pltpu.VMEM((ITERS, peers, count, wide), F32),
            pltpu.VMEM((ITERS, 2, LANES), F32),
            pltpu.VMEM((ITERS, peers, 2, LANES), F32),
            dma((2,)), dma((2,)), dma((2, 2)), dma((2, 2)),
            dma((ITERS, peers)), dma((ITERS, peers)), dma((ITERS, peers)), dma((ITERS, peers)),
            pltpu.SemaphoreType.REGULAR((max(n.bit_length() - 1, 1),)),
            pltpu.VMEM((2,) + skeleton.shape, F32),
            pltpu.VMEM((2,) + transfer.shape, F32),
            pltpu.VMEM((2, 8, LANES), F32),
            pltpu.VMEM(transfer.shape, F32),
            pltpu.VMEM((8, LANES), F32),
            pltpu.VMEM((2, wide, points), BF),
            pltpu.VMEM((2, wide, points), BF),
            dma((3, 2)), dma((3, 2)),
        ],
        compiler_params=pltpu.CompilerParams(
            collective_id=0, has_side_effects=True, vmem_limit_bytes=60 * 1024 * 1024
        ),
    )(coords, skeleton, transfer, coupling, parent, near_mask, noise.reshape(1, points), rhs)


def solution(mesh):
    return jax.shard_map(
        per_device,
        mesh=mesh,
        in_specs=(
            P(None, "leaf"),
            P(None, "leaf"),
            P("leaf", None, None),
            P(),
            P("leaf"),
            P("leaf", None),
            P("leaf"),
            P("rep", "leaf"),
        ),
        out_specs=(P("rep", "leaf"), P("rep", "leaf")),
        check_vma=False,
    )
```
